256 devices in a mesh: rep: 16 (over x, z_lo, core), tp: 16 (over z_hi, y).
Axes of the slice: x: 4, y: 4, z: 8 (z_hi: 4, z_lo: 2; z = z_hi * 2 + z_lo), core: 2. Of those that a mesh axis runs over, the one named last changes fastest.
Arguments:
- activations: bfloat16 [16, 256, 2560], P('rep', 'tp'), may hold values from -6 to 6
- out_grad: bfloat16 [16, 256, 2560], P('rep', 'tp'), may hold values from -6 to 6
- gate_weight: bfloat16 [16, 2560, 6912], P('rep', None, 'tp'), may hold values from -6 to 6
- up_weight: bfloat16 [16, 2560, 6912], P('rep', None, 'tp'), may hold values from -6 to 6
- down_weight: bfloat16 [16, 6912, 2560], P('rep', 'tp'), may hold values from -6 to 6
- step_index: int32 [1], replicated, may hold values from 0 to 999
Outputs:
- layer_out: bfloat16 [16, 256, 2560], P('rep', 'tp')
- grad_in: bfloat16 [16, 256, 2560], P('rep', 'tp')
- new_gate: bfloat16 [16, 2560, 6912], P('rep', None, 'tp')
- new_up: bfloat16 [16, 2560, 6912], P('rep', None, 'tp')
- new_down: bfloat16 [16, 6912, 2560], P('rep', 'tp')
The draws below stay inside these ranges and needn't reach their ends.
All inputs are finite; a program needn't handle non-finite values.
Results may differ from the reference program's by a relative error of at most 0.0052.
Values may be sent and summed in bfloat16 or wider, within the bound.
A program may use at most 128 MiB of HBM per device.

```python
import math
import jax
import jax.numpy as jnp
from jax import lax

D = 2560
FF = 6912
TOK = 256
REPS = 16


def block_levels(own_key, shape, cuts, least, top_value):
    level, own = 1.0, jax.random.fold_in(own_key, 6)
    for axis_at, parts in cuts:
        heights = jnp.exp(jax.random.uniform(jax.random.fold_in(own, axis_at), (parts,), jnp.float32, least / len(cuts), top_value / len(cuts)))
        level = level * jnp.repeat(heights, shape[axis_at] // parts).reshape([-1 if axis == axis_at else 1 for axis in range(len(shape))])
    return level


def scatter_about(stream_key, dims, width, limit, cuts=(), held_as=jnp.bfloat16):
    loudness = block_levels(stream_key, dims, cuts, -0.22, 0.18) if cuts else 1.0
    result = jax.random.normal(stream_key, dims, jnp.float32) * width * loudness
    return jnp.minimum(jnp.maximum(result, -limit), limit).astype(held_as)


def setup_inputs(seed: int = 0) -> dict:
    keys = jax.random.split(jax.random.key(seed), 7)
    return {
        "activations": scatter_about(keys[0], (REPS, TOK, D), 1.0, 6.0, ((0, 16), (1, 16))),
        "out_grad": scatter_about(keys[1], (REPS, TOK, D), 1.0, 6.0, ((0, 16), (1, 16))),
        "gate_weight": scatter_about(keys[2], (REPS, D, FF), 1.0, 6.0, ((0, 16), (2, 16))),
        "up_weight": scatter_about(keys[3], (REPS, D, FF), 1.0, 6.0, ((0, 16), (2, 16))),
        "down_weight": scatter_about(keys[4], (REPS, FF, D), 1.0, 6.0, ((0, 16), (1, 16))),
        "step_index": jax.random.randint(keys[5], (1,), 0, 1000).astype(jnp.int32),
    }


def replica_step(operands):
    tokens_in, grads_out, gate_w, up_w, down_w = operands
    width_scale = 1.0 / math.sqrt(D)
    hidden_scale = 1.0 / math.sqrt(FF)
    gate_pre = jnp.dot(tokens_in, gate_w, preferred_element_type=jnp.float32) * width_scale
    up_pre = jnp.dot(tokens_in, up_w, preferred_element_type=jnp.float32) * width_scale
    sigmoid_gate = jax.nn.sigmoid(gate_pre)
    activated = gate_pre * sigmoid_gate
    hidden = (activated * up_pre).astype(jnp.bfloat16)
    layer_out = (jnp.dot(hidden, down_w, preferred_element_type=jnp.float32) * hidden_scale).astype(jnp.bfloat16)
    d_hidden = jnp.dot(grads_out, down_w.T, preferred_element_type=jnp.float32) * hidden_scale
    d_gate = (d_hidden * up_pre * (sigmoid_gate * (1.0 + gate_pre * (1.0 - sigmoid_gate)))).astype(jnp.bfloat16)
    d_up = (d_hidden * activated).astype(jnp.bfloat16)
    grad_down = jnp.dot(hidden.T, grads_out, preferred_element_type=jnp.float32) * hidden_scale
    grad_gate = jnp.dot(tokens_in.T, d_gate, preferred_element_type=jnp.float32) * width_scale
    grad_upw = jnp.dot(tokens_in.T, d_up, preferred_element_type=jnp.float32) * width_scale
    grad_in = ((jnp.dot(d_gate, gate_w.T, preferred_element_type=jnp.float32) + jnp.dot(d_up, up_w.T, preferred_element_type=jnp.float32)) * width_scale).astype(jnp.bfloat16)
    stepped_gate = (gate_w.astype(jnp.float32) - 0.8 * grad_gate).astype(jnp.bfloat16)
    stepped_up = (up_w.astype(jnp.float32) - 0.8 * grad_upw).astype(jnp.bfloat16)
    stepped_down = (down_w.astype(jnp.float32) - 0.8 * grad_down).astype(jnp.bfloat16)
    return (layer_out, grad_in, stepped_gate, stepped_up, stepped_down)

def reference(activations, out_grad, gate_weight, up_weight, down_weight, step_index):
    layer_out, grad_in, stepped_gate, stepped_up, stepped_down = lax.map(replica_step, (activations, out_grad, gate_weight, up_weight, down_weight))
    levels = REPS.bit_length() - 1
    shift_bits = (step_index[0] % levels).astype(jnp.int32)
    distance = jnp.left_shift(jnp.ones((), jnp.int32), shift_bits)

    def average(stepped):
        received = jnp.roll(stepped, distance, axis=0)
        return ((stepped.astype(jnp.float32) + received.astype(jnp.float32)) * 0.5).astype(jnp.bfloat16)
    return (layer_out, grad_in, average(stepped_gate), average(stepped_up), average(stepped_down))
```

```python
from functools import partial
import math

import jax
import jax.numpy as jnp
from jax import lax
from jax.experimental import pallas as pl
from jax.experimental.pallas import tpu as pltpu
from jax.sharding import PartitionSpec as P

D = 2560
FF = 6912
TOK = 256
TP = 16
F = FF // TP
ROWS = TOK // TP

LEARN_RATE = 0.8
WIDTH_SCALE = 1.0 / math.sqrt(D)
HIDDEN_SCALE = 1.0 / math.sqrt(FF)

CHUNK = 512
CHUNKS = D // CHUNK

MESH = pl.DeviceIdType.MESH
BF = jnp.bfloat16
F32 = jnp.float32


def rows_of(block, size):
    return pl.ds(pl.multiple_of(block * size, size), size)


def kernel(
    dist,
    acts_in, grads_in, gate_in, up_in, down_in,
    layer_out, gradin_out, gate_out, up_out, down_out,
    acts, grads, gate_w, up_w, down_w,
    st_gate, st_up, st_down,
    rc_gate, rc_up, rc_down,
    pre_g, pre_u, hid, d_gate, d_up,
    part_l, part_g, ry_l, ry_g, sz_l, sz_g, rz_l, rz_g, fin,
    load_sem, ag_recv, agz_send, agy_send,
    ex_send, ex_recv, ry_send, ry_recv, rz_send, rz_recv, out_sem,
):
    rep = lax.axis_index("rep")
    tp = lax.axis_index("tp")
    zh, y = tp // 4, lax.rem(tp, 4)

    def z_peer(k):
        return (rep, lax.rem(zh + k, 4) * 4 + y)

    def y_peer(k):
        return (rep, zh * 4 + lax.rem(y + k, 4))

    to_partner = (lax.rem(rep + dist, 16), tp)
    from_partner = (lax.rem(rep + 16 - dist, 16), tp)

    loads = [
        pltpu.make_async_copy(gate_in, gate_w, load_sem.at[0]),
        pltpu.make_async_copy(up_in, up_w, load_sem.at[1]),
        pltpu.make_async_copy(down_in, down_w, load_sem.at[2]),
    ]
    own = rows_of(y * 4 + zh, ROWS)
    own_loads = [
        pltpu.make_async_copy(acts_in, acts.at[own], load_sem.at[3]),
        pltpu.make_async_copy(grads_in, grads.at[own], load_sem.at[4]),
    ]

    barrier = pltpu.get_barrier_semaphore()
    friends = [z_peer(k) for k in (1, 2, 3)] + [y_peer(k) for k in (1, 2, 3)] + [to_partner]
    if dist != 8:
        friends.append(from_partner)
    for friend in friends:
        pl.semaphore_signal(barrier, inc=1, device_id=friend, device_id_type=MESH)
    for copy in own_loads + loads:
        copy.start()
    pl.semaphore_wait(barrier, len(friends))

    sources = ((acts_in, acts), (grads_in, grads))

    def z_copy(a, k):
        src, dst = sources[a]
        b = y * 4 + zh
        return pltpu.make_async_remote_copy(
            src, dst.at[rows_of(b, ROWS)], agz_send.at[a, k - 1], ag_recv.at[a, b],
            device_id=z_peer(k), device_id_type=MESH)

    def y_copy(a, j, k):
        src, dst = sources[a]
        b = y * 4 + lax.rem(zh + 4 - j, 4)
        return pltpu.make_async_remote_copy(
            src if j == 0 else dst.at[rows_of(b, ROWS)], dst.at[rows_of(b, ROWS)],
            agy_send.at[a, j, k - 1], ag_recv.at[a, b],
            device_id=y_peer(k), device_id_type=MESH)

    def arrived(a, b):
        src, dst = sources[a]
        pltpu.make_async_remote_copy(
            src, dst.at[rows_of(b, ROWS)], agz_send.at[a, 0], ag_recv.at[a, b],
            device_id=z_peer(1), device_id_type=MESH).wait_recv()

    order = (1, 3, 2)
    for k in order:
        z_copy(0, k).start()
    for k in order:
        y_copy(0, 0, k).start()
    for k in order:
        z_copy(1, k).start()
    for k in order:
        y_copy(1, 0, k).start()
    for a in (0, 1):
        for j in order:
            arrived(a, y * 4 + lax.rem(zh + 4 - j, 4))
            for k in order:
                y_copy(a, j, k).start()

    def rest_arrived(a):
        for k in order:
            for j in (0,) + order:
                arrived(a, lax.rem(y + 4 - k, 4) * 4 + lax.rem(zh + 4 - j, 4))

    rest_arrived(0)
    own_loads[0].wait()
    loads[0].wait()
    pre_g[...] = jnp.dot(acts[...], gate_w[...], preferred_element_type=F32) * WIDTH_SCALE
    loads[1].wait()
    pre_u[...] = jnp.dot(acts[...], up_w[...], preferred_element_type=F32) * WIDTH_SCALE

    def make_hidden(i, _):
        r = rows_of(i, 32)
        g = pre_g[r, :]
        hid[r, :] = (g * jax.nn.sigmoid(g) * pre_u[r, :]).astype(BF)
        return 0

    lax.fori_loop(0, TOK // 32, make_hidden, 0)

    rest_arrived(1)
    own_loads[1].wait()
    loads[2].wait()

    def ex_copy(m, c):
        st, rc = ((st_down, rc_down), (st_gate, rc_gate), (st_up, rc_up))[m]
        piece = pl.ds(pl.multiple_of(c * CHUNK, CHUNK), CHUNK)
        at = (slice(None), piece) if m == 0 else (piece, slice(None))
        return pltpu.make_async_remote_copy(
            st.at[at], rc.at[at], ex_send.at[m, c], ex_recv.at[m, c],
            device_id=to_partner, device_id_type=MESH)

    def step_down(c, _):
        piece = pl.ds(pl.multiple_of(c * CHUNK, CHUNK), CHUNK)
        g = lax.dot_general(hid[...], grads[:, piece], (((0,), (0,)), ((), ())), preferred_element_type=F32)
        st_down[:, piece] = (down_w[:, piece].astype(F32) - (LEARN_RATE * HIDDEN_SCALE) * g).astype(BF)
        ex_copy(0, c).start()
        return 0

    lax.fori_loop(0, CHUNKS, step_down, 0)

    d_hid = lax.dot_general(grads[...], down_w[...], (((1,), (1,)), ((), ())), preferred_element_type=F32)
    fin[...] = d_hid * HIDDEN_SCALE

    def make_d(i, _):
        r = rows_of(i, 32)
        g = pre_g[r, :]
        s = jax.nn.sigmoid(g)
        d = fin[r, :]
        d_gate[r, :] = (d * pre_u[r, :] * (s * (1.0 + g * (1.0 - s)))).astype(BF)
        d_up[r, :] = (d * (g * s)).astype(BF)
        return 0

    lax.fori_loop(0, TOK // 32, make_d, 0)

    def step_wide(m, w, st, dd, c):
        piece = pl.ds(pl.multiple_of(c * CHUNK, CHUNK), CHUNK)
        g = lax.dot_general(acts[:, piece], dd[...], (((0,), (0,)), ((), ())), preferred_element_type=F32)
        st[piece, :] = (w[piece, :].astype(F32) - (LEARN_RATE * WIDTH_SCALE) * g).astype(BF)
        ex_copy(m, c).start()

    def step_gate(c, _):
        step_wide(1, gate_w, st_gate, d_gate, c)
        return 0

    def step_up(c, _):
        step_wide(2, up_w, st_up, d_up, c)
        return 0

    lax.fori_loop(0, CHUNKS, step_gate, 0)
    lax.fori_loop(0, CHUNKS, step_up, 0)

    def layer_piece(c, _):
        piece = pl.ds(pl.multiple_of(c * CHUNK, CHUNK), CHUNK)
        part_l[:, piece] = (
            jnp.dot(hid[...], down_w[:, piece], preferred_element_type=F32) * HIDDEN_SCALE
        ).astype(BF)
        return 0

    def gradin_piece(c, _):
        piece = pl.ds(pl.multiple_of(c * CHUNK, CHUNK), CHUNK)
        nt = (((1,), (1,)), ((), ()))
        total = lax.dot_general(d_gate[...], gate_w[piece, :], nt, preferred_element_type=F32)
        total += lax.dot_general(d_up[...], up_w[piece, :], nt, preferred_element_type=F32)
        part_g[:, piece] = (total * WIDTH_SCALE).astype(BF)
        return 0

    sums = ((part_l, ry_l, sz_l, rz_l, layer_out), (part_g, ry_g, sz_g, rz_g, gradin_out))

    def ry_copy(a, k):
        part, ry = sums[a][:2]
        return pltpu.make_async_remote_copy(
            part.at[rows_of(lax.rem(y + k, 4), 64)], ry.at[k - 1], ry_send.at[a, k - 1], ry_recv.at[a, k - 1],
            device_id=y_peer(k), device_id_type=MESH)

    def rz_copy(a, k):
        sz, rz = sums[a][2:4]
        return pltpu.make_async_remote_copy(
            sz.at[rows_of(lax.rem(zh + k, 4), ROWS)], rz.at[k - 1], rz_send.at[a, k - 1], rz_recv.at[a, k - 1],
            device_id=z_peer(k), device_id_type=MESH)

    lax.fori_loop(0, CHUNKS, layer_piece, 0)
    for k in order:
        ry_copy(0, k).start()
    lax.fori_loop(0, CHUNKS, gradin_piece, 0)
    for k in order:
        ry_copy(1, k).start()

    for a in (0, 1):
        part, ry, sz = sums[a][:3]
        for k in order:
            ry_copy(a, k).wait_recv()

        def sum_y(i, _):
            r = rows_of(i, 16)
            mine = part[rows_of(y * 4 + i, 16), :].astype(F32)
            sz[r, :] = (
                (mine + ry[0, r, :].astype(F32)) + (ry[1, r, :].astype(F32) + ry[2, r, :].astype(F32))
            ).astype(BF)
            return 0

        lax.fori_loop(0, 4, sum_y, 0)
        for k in order:
            rz_copy(a, k).start()

    def average(m, c):
        st, rc, out = ((st_down, rc_down, down_out), (st_gate, rc_gate, gate_out), (st_up, rc_up, up_out))[m]
        piece = pl.ds(pl.multiple_of(c * CHUNK, CHUNK), CHUNK)
        at = (slice(None), piece) if m == 0 else (piece, slice(None))
        ex_copy(m, c).wait_recv()
        rc[at] = ((st[at].astype(F32) + rc[at].astype(F32)) * 0.5).astype(BF)
        pltpu.make_async_copy(rc.at[at], out.at[at], out_sem.at[m, c]).start()
        return 0

    lax.fori_loop(0, CHUNKS, lambda c, _: average(0, c), 0)

    for a in (0, 1):
        part, ry, sz, rz, out = sums[a]
        for k in order:
            rz_copy(a, k).wait_recv()
        total = sz[rows_of(zh, ROWS), :].astype(F32)
        for k in (0, 1, 2):
            total += rz[k].astype(F32)
        sz[rows_of(zh, ROWS), :] = total.astype(BF)
        pltpu.make_async_copy(sz.at[rows_of(zh, ROWS)], out, load_sem.at[3 + a]).start()

    lax.fori_loop(0, CHUNKS, lambda c, _: average(1, c), 0)
    lax.fori_loop(0, CHUNKS, lambda c, _: average(2, c), 0)

    for a in (0, 1):
        for k in order:
            z_copy(a, k).wait_send()
            for j in (0, 1, 2, 3):
                y_copy(a, j, k).wait_send()
            ry_copy(a, k).wait_send()
            rz_copy(a, k).wait_send()
        sz, out = sums[a][2], sums[a][4]
        pltpu.make_async_copy(sz.at[rows_of(zh, ROWS)], out, load_sem.at[3 + a]).wait()

    def finish(m, c):
        rc, out = ((rc_down, down_out), (rc_gate, gate_out), (rc_up, up_out))[m]
        piece = pl.ds(pl.multiple_of(c * CHUNK, CHUNK), CHUNK)
        at = (slice(None), piece) if m == 0 else (piece, slice(None))
        ex_copy(m, c).wait_send()
        pltpu.make_async_copy(rc.at[at], out.at[at], out_sem.at[m, c]).wait()
        return 0

    for m in (0, 1, 2):
        lax.fori_loop(0, CHUNKS, lambda c, _: finish(m, c), 0)


def step(level, acts, grads, gate_w, up_w, down_w):
    any_spec = pl.BlockSpec(memory_space=pl.ANY)
    vm = pltpu.VMEM
    dma = pltpu.SemaphoreType.DMA
    wide, tall, full = (D, F), (F, D), (TOK, D)
    return pl.pallas_call(
        partial(kernel, 1 << level),
        out_shape=(
            jax.ShapeDtypeStruct((ROWS, D), BF),
            jax.ShapeDtypeStruct((ROWS, D), BF),
            jax.ShapeDtypeStruct(wide, BF),
            jax.ShapeDtypeStruct(wide, BF),
            jax.ShapeDtypeStruct(tall, BF),
        ),
        in_specs=[any_spec] * 5,
        out_specs=(any_spec,) * 5,
        scratch_shapes=[
            vm(full, BF), vm(full, BF), vm(wide, BF), vm(wide, BF), vm(tall, BF),
            vm(wide, BF), vm(wide, BF), vm(tall, BF),
            vm(wide, BF), vm(wide, BF), vm(tall, BF),
            vm((TOK, F), F32), vm((TOK, F), F32), vm((TOK, F), BF), vm((TOK, F), BF), vm((TOK, F), BF),
            vm(full, BF), vm(full, BF),
            vm((3, 64, D), BF), vm((3, 64, D), BF), vm((64, D), BF), vm((64, D), BF),
            vm((3, ROWS, D), BF), vm((3, ROWS, D), BF), vm((TOK, F), F32),
            dma((5,)), dma((2, 16)), dma((2, 3)), dma((2, 4, 3)),
            dma((3, CHUNKS)), dma((3, CHUNKS)),
            dma((2, 3)), dma((2, 3)), dma((2, 3)), dma((2, 3)), dma((3, CHUNKS)),
        ],
        compiler_params=pltpu.CompilerParams(
            collective_id=level, has_side_effects=True, vmem_limit_bytes=60 * 1024 * 1024),
        name=f"gossip_step_{1 << level}",
    )(acts, grads, gate_w, up_w, down_w)


def shards(activations, out_grad, gate_weight, up_weight, down_weight, step_index):
    level = step_index[0] % 4
    outs = lax.switch(
        level,
        [partial(step, i) for i in range(4)],
        activations[0], out_grad[0], gate_weight[0], up_weight[0], down_weight[0],
    )
    return tuple(o[None] for o in outs)


def solution(mesh):
    in_specs = (
        P("rep", "tp", None),
        P("rep", "tp", None),
        P("rep", None, "tp"),
        P("rep", None, "tp"),
        P("rep", "tp", None),
        P(),
    )
    out_specs = (
        P("rep", "tp", None),
        P("rep", "tp", None),
        P("rep", None, "tp"),
        P("rep", None, "tp"),
        P("rep", "tp", None),
    )
    return jax.shard_map(shards, mesh=mesh, in_specs=in_specs, out_specs=out_specs, check_vma=False)
```

```python
from functools import partial
import math

import jax
import jax.numpy as jnp
from jax import lax
from jax.experimental import pallas as pl
from jax.experimental.pallas import tpu as pltpu
from jax.sharding import PartitionSpec as P

D = 2560
FF = 6912
TOK = 256
TP = 16
F = FF // TP
ROWS = TOK // TP

LEARN_RATE = 0.8
WIDTH_SCALE = 1.0 / math.sqrt(D)
HIDDEN_SCALE = 1.0 / math.sqrt(FF)

CHUNK = 512
CHUNKS = D // CHUNK
WCHUNK = 256
WCHUNKS = D // WCHUNK

MESH = pl.DeviceIdType.MESH
BF = jnp.bfloat16
F32 = jnp.float32

NT = (((1,), (1,)), ((), ()))
TN = (((0,), (0,)), ((), ()))


def rows_of(block, size):
    return pl.ds(pl.multiple_of(block * size, size), size)


def dot(a, b):
    return jnp.dot(a, b, preferred_element_type=F32)


def kernel(
    dist,
    acts_in, grads_in, gate_in, up_in, down_in,
    layer_out, gradin_out, gate_out, up_out, down_out,
    acts, grads, pgrads, wide, down,
    st_wide, st_down, rc_wide, rc_down,
    pre, dhid, hid, phid, dd,
    part_l, part_g, ry_l, ry_g, sz_l, sz_g, rz_l, rz_g,
    load_sem, ag_recv, agz_send, agy_send, shard_send,
    raw_send, raw_recv, hid_send, hid_recv, ex_send, ex_recv,
    ry_send, ry_recv, rz_send, rz_recv, down_sem, wide_sem,
):
    rep = lax.axis_index("rep")
    tp = lax.axis_index("tp")
    zh, y = tp // 4, lax.rem(tp, 4)
    order = (1, 3, 2)

    def z_peer(k):
        return (rep, lax.rem(zh + k, 4) * 4 + y)

    def y_peer(k):
        return (rep, zh * 4 + lax.rem(y + k, 4))

    to_partner = (lax.rem(rep + dist, 16), tp)
    from_partner = (lax.rem(rep + 16 - dist, 16), tp)

    def send(src, dst, send_sem, recv_sem, device):
        return pltpu.make_async_remote_copy(
            src, dst, send_sem, recv_sem, device_id=device, device_id_type=MESH)

    loads = [
        pltpu.make_async_copy(gate_in, wide.at[pl.ds(0, F)], load_sem.at[0]),
        pltpu.make_async_copy(up_in, wide.at[pl.ds(F, F)], load_sem.at[1]),
        pltpu.make_async_copy(down_in, down, load_sem.at[2]),
    ]
    own_block = y * 4 + zh
    own = rows_of(own_block, ROWS)
    own_loads = [
        pltpu.make_async_copy(acts_in, acts.at[own], load_sem.at[3]),
        pltpu.make_async_copy(grads_in, grads.at[own], load_sem.at[4]),
    ]

    barrier = pltpu.get_barrier_semaphore()
    friends = [z_peer(k) for k in (1, 2, 3)] + [y_peer(k) for k in (1, 2, 3)] + [to_partner]
    if dist != 8:
        friends.append(from_partner)
    for friend in friends:
        pl.semaphore_signal(barrier, inc=1, device_id=friend, device_id_type=MESH)
    for copy in own_loads + loads:
        copy.start()
    pl.semaphore_wait(barrier, len(friends))

    sources = ((acts_in, acts), (grads_in, grads), (pgrads.at[own], pgrads))

    def z_copy(a, k):
        src, dst = sources[a]
        return send(src, dst.at[own], agz_send.at[a, k - 1], ag_recv.at[a, own_block], z_peer(k))

    def y_copy(a, j, k):
        src, dst = sources[a]
        b = y * 4 + lax.rem(zh + 4 - j, 4)
        rows = dst.at[rows_of(b, ROWS)]
        return send(src if j == 0 else rows, rows, agy_send.at[a, j, k - 1], ag_recv.at[a, b], y_peer(k))

    def arrived(a, b):
        src, dst = sources[a]
        send(dst.at[rows_of(b, ROWS)], dst.at[rows_of(b, ROWS)], agz_send.at[a, 0], ag_recv.at[a, b],
             z_peer(1)).wait_recv()

    def z_start(a):
        for k in order:
            z_copy(a, k).start()

    def y_start(a, j):
        for k in order:
            y_copy(a, j, k).start()

    def z_forward(a):
        for j in order:
            arrived(a, y * 4 + lax.rem(zh + 4 - j, 4))
            y_start(a, j)

    def rest_arrived(a):
        for k in order:
            for j in (0,) + order:
                arrived(a, lax.rem(y + 4 - k, 4) * 4 + lax.rem(zh + 4 - j, 4))

    shard_copy = send(grads_in, pgrads.at[own], shard_send, ag_recv.at[2, own_block], to_partner)
    hid_copy = send(hid, phid, hid_send, hid_recv, to_partner)

    def raw_copy(c):
        piece = rows_of(c, CHUNK)
        return send(down_in.at[:, piece], rc_down.at[:, piece], raw_send.at[c], raw_recv.at[c], to_partner)

    def ex_copy(c):
        piece = rows_of(c, WCHUNK)
        return send(st_wide.at[:, piece], rc_wide.at[:, piece], ex_send.at[c], ex_recv.at[c], to_partner)

    def start_raw():
        def one(c, _):
            raw_copy(c).start()
            return 0
        lax.fori_loop(0, CHUNKS, one, 0)

    z_start(0)
    y_start(0, 0)
    z_start(1)
    y_start(1, 0)
    shard_copy.start()
    if dist > 2:
        start_raw()
    z_forward(0)
    z_forward(1)
    arrived(2, own_block)
    z_start(2)
    y_start(2, 0)
    if dist <= 2:
        start_raw()

    rest_arrived(0)
    own_loads[0].wait()
    loads[0].wait()
    loads[1].wait()
    pre[...] = lax.dot_general(wide[...], acts[...], NT, preferred_element_type=F32) * WIDTH_SCALE

    def make_hidden(i, _):
        r = rows_of(i, 16)
        g = pre[r, :]
        u = pre[pl.ds(pl.multiple_of(F + i * 16, 16), 16), :]
        hid[r, :] = (g * jax.nn.sigmoid(g) * u).astype(BF)
        return 0

    lax.fori_loop(0, F // 16, make_hidden, 0)
    hid_copy.start()

    loads[2].wait()

    def layer_piece(c, _):
        piece = rows_of(c, CHUNK)
        part_l[:, piece] = (
            lax.dot_general(hid[...], down[:, piece], TN, preferred_element_type=F32) * HIDDEN_SCALE
        ).astype(BF)
        return 0

    lax.fori_loop(0, CHUNKS, layer_piece, 0)

    rest_arrived(1)
    own_loads[1].wait()

    dhid[...] = lax.dot_general(down[...], grads[...], NT, preferred_element_type=F32) * HIDDEN_SCALE

    def make_d(i, _):
        r = rows_of(i, 16)
        ru = pl.ds(pl.multiple_of(F + i * 16, 16), 16)
        g = pre[r, :]
        u = pre[ru, :]
        s = jax.nn.sigmoid(g)
        d = dhid[r, :]
        dd[r, :] = (d * u * (s * (1.0 + g * (1.0 - s)))).astype(BF)
        dd[ru, :] = (d * (g * s)).astype(BF)
        return 0

    lax.fori_loop(0, F // 16, make_d, 0)

    def step_wide(c, _):
        piece = rows_of(c, WCHUNK)
        g = dot(dd[...], acts[:, piece])
        st_wide[:, piece] = (wide[:, piece].astype(F32) - (LEARN_RATE * WIDTH_SCALE) * g).astype(BF)
        ex_copy(c).start()
        return 0

    lax.fori_loop(0, WCHUNKS, step_wide, 0)

    sums = ((part_l, ry_l, sz_l, rz_l, layer_out), (part_g, ry_g, sz_g, rz_g, gradin_out))

    def ry_copy(a, k):
        part, ry = sums[a][:2]
        return send(part.at[rows_of(lax.rem(y + k, 4), 64)], ry.at[k - 1],
                    ry_send.at[a, k - 1], ry_recv.at[a, k - 1], y_peer(k))

    def rz_copy(a, k):
        sz, rz = sums[a][2:4]
        return send(sz.at[rows_of(lax.rem(zh + k, 4), ROWS)], rz.at[k - 1],
                    rz_send.at[a, k - 1], rz_recv.at[a, k - 1], z_peer(k))

    for k in order:
        ry_copy(0, k).start()

    def gradin_piece(c, _):
        piece = rows_of(c, CHUNK)
        part_g[:, piece] = (
            lax.dot_general(dd[...], wide[:, piece], TN, preferred_element_type=F32) * WIDTH_SCALE
        ).astype(BF)
        return 0

    lax.fori_loop(0, CHUNKS, gradin_piece, 0)
    for k in order:
        ry_copy(1, k).start()

    z_forward(2)

    def step_of(w, h, g, piece):
        return (w[:, piece].astype(F32) - (LEARN_RATE * HIDDEN_SCALE) * dot(h[...], g[:, piece])).astype(BF)

    def step_down(c, _):
        piece = rows_of(c, CHUNK)
        st_down[:, piece] = step_of(down, hid, grads, piece)
        return 0

    lax.fori_loop(0, CHUNKS, step_down, 0)

    for a in (0, 1):
        part, ry, sz = sums[a][:3]
        for k in order:
            ry_copy(a, k).wait_recv()

        def sum_y(i, _):
            r = rows_of(i, 16)
            mine = part[rows_of(y * 4 + i, 16), :].astype(F32)
            sz[r, :] = (
                (mine + ry[0, r, :].astype(F32)) + (ry[1, r, :].astype(F32) + ry[2, r, :].astype(F32))
            ).astype(BF)
            return 0

        lax.fori_loop(0, 4, sum_y, 0)
        for k in order:
            rz_copy(a, k).start()

    rest_arrived(2)
    hid_copy.wait_recv()

    def down_write(c):
        piece = rows_of(c, CHUNK)
        return pltpu.make_async_copy(rc_down.at[:, piece], down_out.at[:, piece], down_sem.at[c])

    def average_down(c, _):
        piece = rows_of(c, CHUNK)
        raw_copy(c).wait_recv()
        theirs = step_of(rc_down, phid, pgrads, piece).astype(F32)
        rc_down[:, piece] = ((st_down[:, piece].astype(F32) + theirs) * 0.5).astype(BF)
        down_write(c).start()
        return 0

    lax.fori_loop(0, CHUNKS, average_down, 0)

    def sum_write(a):
        return pltpu.make_async_copy(sums[a][2].at[rows_of(zh, ROWS)], sums[a][4], load_sem.at[3 + a])

    for a in (0, 1):
        sz, rz = sums[a][2:4]
        for k in order:
            rz_copy(a, k).wait_recv()
        total = sz[rows_of(zh, ROWS), :].astype(F32)
        for k in (0, 1, 2):
            total += rz[k].astype(F32)
        sz[rows_of(zh, ROWS), :] = total.astype(BF)
        sum_write(a).start()

    def wide_write(h, c):
        piece = rows_of(c, WCHUNK)
        return pltpu.make_async_copy(
            rc_wide.at[pl.ds(h * F, F), piece], (gate_out, up_out)[h].at[:, piece], wide_sem.at[h, c])

    def average_wide(c, _):
        piece = rows_of(c, WCHUNK)
        ex_copy(c).wait_recv()
        rc_wide[:, piece] = ((st_wide[:, piece].astype(F32) + rc_wide[:, piece].astype(F32)) * 0.5).astype(BF)
        wide_write(0, c).start()
        wide_write(1, c).start()
        return 0

    lax.fori_loop(0, WCHUNKS, average_wide, 0)

    for a in (0, 1, 2):
        for k in order:
            z_copy(a, k).wait_send()
            for j in (0, 1, 2, 3):
                y_copy(a, j, k).wait_send()
    for a in (0, 1):
        for k in order:
            ry_copy(a, k).wait_send()
            rz_copy(a, k).wait_send()
        sum_write(a).wait()
    shard_copy.wait_send()
    hid_copy.wait_send()

    def finish_down(c, _):
        raw_copy(c).wait_send()
        down_write(c).wait()
        return 0

    def finish_wide(c, _):
        ex_copy(c).wait_send()
        wide_write(0, c).wait()
        wide_write(1, c).wait()
        return 0

    lax.fori_loop(0, CHUNKS, finish_down, 0)
    lax.fori_loop(0, WCHUNKS, finish_wide, 0)


def step(level, acts, grads, gate_w, up_w, down_w):
    any_spec = pl.BlockSpec(memory_space=pl.ANY)
    vm = pltpu.VMEM
    dma = pltpu.SemaphoreType.DMA
    tall, stack, full, hidden = (F, D), (2 * F, D), (TOK, D), (F, TOK)
    return pl.pallas_call(
        partial(kernel, 1 << level),
        out_shape=(
            jax.ShapeDtypeStruct((ROWS, D), BF),
            jax.ShapeDtypeStruct((ROWS, D), BF),
            jax.ShapeDtypeStruct(tall, BF),
            jax.ShapeDtypeStruct(tall, BF),
            jax.ShapeDtypeStruct(tall, BF),
        ),
        in_specs=[any_spec] * 5,
        out_specs=(any_spec,) * 5,
        scratch_shapes=[
            vm(full, BF), vm(full, BF), vm(full, BF), vm(stack, BF), vm(tall, BF),
            vm(stack, BF), vm(tall, BF), vm(stack, BF), vm(tall, BF),
            vm((2 * F, TOK), F32), vm(hidden, F32), vm(hidden, BF), vm(hidden, BF), vm((2 * F, TOK), BF),
            vm(full, BF), vm(full, BF),
            vm((3, 64, D), BF), vm((3, 64, D), BF), vm((64, D), BF), vm((64, D), BF),
            vm((3, ROWS, D), BF), vm((3, ROWS, D), BF),
            dma((5,)), dma((3, 16)), dma((3, 3)), dma((3, 4, 3)), dma,
            dma((CHUNKS,)), dma((CHUNKS,)), dma, dma, dma((WCHUNKS,)), dma((WCHUNKS,)),
            dma((2, 3)), dma((2, 3)), dma((2, 3)), dma((2, 3)), dma((CHUNKS,)), dma((2, WCHUNKS)),
        ],
        compiler_params=pltpu.CompilerParams(
            collective_id=level, has_side_effects=True, vmem_limit_bytes=60 * 1024 * 1024),
        name=f"gossip_step_{1 << level}",
    )(acts, grads, gate_w, up_w, down_w)


def shards(activations, out_grad, gate_weight, up_weight, down_weight, step_index):
    level = step_index[0] % 4
    outs = lax.switch(
        level,
        [partial(step, i) for i in range(4)],
        activations[0], out_grad[0], gate_weight[0].T, up_weight[0].T, down_weight[0],
    )
    return outs[0][None], outs[1][None], outs[2].T[None], outs[3].T[None], outs[4][None]


def solution(mesh):
    in_specs = (
        P("rep", "tp", None),
        P("rep", "tp", None),
        P("rep", None, "tp"),
        P("rep", None, "tp"),
        P("rep", "tp", None),
        P(),
    )
    out_specs = (
        P("rep", "tp", None),
        P("rep", "tp", None),
        P("rep", None, "tp"),
        P("rep", None, "tp"),
        P("rep", "tp", None),
    )
    return jax.shard_map(shards, mesh=mesh, in_specs=in_specs, out_specs=out_specs, check_vma=False)
```

```python
from functools import partial
import math

import jax
import jax.numpy as jnp
from jax import lax
from jax.experimental import pallas as pl
from jax.experimental.pallas import tpu as pltpu
from jax.sharding import PartitionSpec as P

D = 2560
FF = 6912
TOK = 256
TP = 16
F = FF // TP
ROWS = TOK // TP

LEARN_RATE = 0.8
WIDTH_SCALE = 1.0 / math.sqrt(D)
HIDDEN_SCALE = 1.0 / math.sqrt(FF)

CHUNK = 256
CHUNKS = D // CHUNK
PIECE = 512
PIECES = D // PIECE
WCHUNK = 256
WCHUNKS = D // WCHUNK
LONG_RAW = 3
LONG_WIDE = 2

KERNEL_VMEM = 56 * 1024 * 1024
EMIT_PARTS = 3
EMIT_ROWS = F // EMIT_PARTS

MESH = pl.DeviceIdType.MESH
BF = jnp.bfloat16
F32 = jnp.float32

NT = (((1,), (1,)), ((), ()))
TN = (((0,), (0,)), ((), ()))


def rows_of(block, size):
    return pl.ds(pl.multiple_of(block * size, size), size)


def dot(a, b):
    return jnp.dot(a, b, preferred_element_type=F32)


def kernel(
    dist,
    acts_in, grads_in, gate_in, up_in, down_in,
    layer_out, gradin_out, gate_out, up_out, down_out,
    acts, grads, pgrads, wide, down,
    st_wide, st_down, rc_wide, rc_down,
    pre, dhid, hid, phid, dd,
    part_l, part_g, ry_l, ry_g, sz_l, sz_g, rz_l, rz_g,
    load_sem, ag_recv, agz_send, agy_send, shard_send,
    raw_send, raw_recv, hid_send, hid_recv, ex_send, ex_recv,
    ry_send, ry_recv, rz_send, rz_recv, down_sem, wide_sem,
    *relay,
):
    rep = lax.axis_index("rep")
    tp = lax.axis_index("tp")
    zh, y = tp // 4, lax.rem(tp, 4)
    order = (1, 3, 2)

    def z_peer(k):
        return (rep, lax.rem(zh + k, 4) * 4 + y)

    def y_peer(k):
        return (rep, zh * 4 + lax.rem(y + k, 4))

    to_partner = (lax.rem(rep + dist, 16), tp)
    from_partner = (lax.rem(rep + 16 - dist, 16), tp)

    def send(src, dst, send_sem, recv_sem, device):
        return pltpu.make_async_remote_copy(
            src, dst, send_sem, recv_sem, device_id=device, device_id_type=MESH)

    loads = [
        pltpu.make_async_copy(gate_in, wide.at[pl.ds(0, F)], load_sem.at[0]),
        pltpu.make_async_copy(up_in, wide.at[pl.ds(F, F)], load_sem.at[1]),
        pltpu.make_async_copy(down_in, down, load_sem.at[2]),
    ]
    own_block = y * 4 + zh
    own = rows_of(own_block, ROWS)
    own_loads = [
        pltpu.make_async_copy(acts_in, acts.at[own], load_sem.at[3]),
        pltpu.make_async_copy(grads_in, grads.at[own], load_sem.at[4]),
    ]

    barrier = pltpu.get_barrier_semaphore()
    friends = [z_peer(k) for k in (1, 2, 3)] + [y_peer(k) for k in (1, 2, 3)] + [to_partner]
    if dist != 8:
        friends.append(from_partner)
    for friend in friends:
        pl.semaphore_signal(barrier, inc=1, device_id=friend, device_id_type=MESH)
    for copy in own_loads + loads:
        copy.start()
    pl.semaphore_wait(barrier, len(friends))

    sources = ((acts_in, acts), (grads_in, grads), (pgrads.at[own], pgrads))

    def z_copy(a, k):
        src, dst = sources[a]
        return send(src, dst.at[own], agz_send.at[a, k - 1], ag_recv.at[a, own_block], z_peer(k))

    def y_copy(a, j, k):
        src, dst = sources[a]
        b = y * 4 + lax.rem(zh + 4 - j, 4)
        rows = dst.at[rows_of(b, ROWS)]
        return send(src if j == 0 else rows, rows, agy_send.at[a, j, k - 1], ag_recv.at[a, b], y_peer(k))

    def arrived(a, b):
        src, dst = sources[a]
        send(dst.at[rows_of(b, ROWS)], dst.at[rows_of(b, ROWS)], agz_send.at[a, 0], ag_recv.at[a, b],
             z_peer(1)).wait_recv()

    def z_start(a):
        for k in order:
            z_copy(a, k).start()

    def y_start(a, j):
        for k in order:
            y_copy(a, j, k).start()

    def z_forward(a):
        for j in order:
            arrived(a, y * 4 + lax.rem(zh + 4 - j, 4))
            y_start(a, j)

    def rest_arrived(a):
        for k in order:
            for j in (0,) + order:
                arrived(a, lax.rem(y + 4 - k, 4) * 4 + lax.rem(zh + 4 - j, 4))

    shard_copy = send(grads_in, pgrads.at[own], shard_send, ag_recv.at[2, own_block], to_partner)
    hid_copy = send(hid, phid, hid_send, hid_recv, to_partner)

    def raw_copy(c):
        piece = rows_of(c, CHUNK)
        return send(down_in.at[:, piece], rc_down.at[:, piece], raw_send.at[c], raw_recv.at[c], to_partner)

    def ex_copy(c):
        piece = rows_of(c, WCHUNK)
        return send(st_wide.at[:, piece], rc_wide.at[:, piece], ex_send.at[c], ex_recv.at[c], to_partner)

    long_raw, long_wide = (LONG_RAW, LONG_WIDE) if dist == 4 else (0, 0)

    def hop(kind, c, n):
        piece = rows_of(c, CHUNK if kind == 0 else WCHUNK)
        raw_a, raw_b, wide_a, wide_b, relay_send, relay_recv = relay
        i = c if kind == 0 else LONG_RAW + c
        a, b = (raw_a.at[c], raw_b.at[c]) if kind == 0 else (wide_a.at[c], wide_b.at[c])
        src, dst = ((down_in, rc_down), (st_wide, rc_wide))[kind]
        first_send, last_recv = ((raw_send, raw_recv), (ex_send, ex_recv))[kind]
        if n == 0:
            return send(src.at[:, piece], a, first_send.at[c], relay_recv.at[0, i], from_partner)
        if n == 1:
            return send(a, b, relay_send.at[0, i], relay_recv.at[1, i], from_partner)
        return send(b, dst.at[:, piece], relay_send.at[1, i], last_recv.at[c], from_partner)

    def pass_on(kind, n):
        for c in range((long_raw, long_wide)[kind]):
            hop(kind, c, n - 1).wait_recv()
            hop(kind, c, n).start()

    def start_raw():
        for c in range(long_raw):
            hop(0, c, 0).start()

        def one(c, _):
            raw_copy(c).start()
            return 0
        lax.fori_loop(long_raw, CHUNKS, one, 0)

    z_start(0)
    y_start(0, 0)
    z_start(1)
    y_start(1, 0)
    shard_copy.start()
    start_raw()
    z_forward(0)
    z_forward(1)
    arrived(2, own_block)
    z_start(2)
    y_start(2, 0)
    pass_on(0, 1)

    rest_arrived(0)
    own_loads[0].wait()
    loads[0].wait()
    loads[1].wait()
    pre[...] = lax.dot_general(wide[...], acts[...], NT, preferred_element_type=F32) * WIDTH_SCALE

    def make_hidden(i, _):
        r = rows_of(i, 16)
        g = pre[r, :]
        u = pre[pl.ds(pl.multiple_of(F + i * 16, 16), 16), :]
        hid[r, :] = (g * jax.nn.sigmoid(g) * u).astype(BF)
        return 0

    lax.fori_loop(0, F // 16, make_hidden, 0)
    hid_copy.start()

    loads[2].wait()

    def layer_piece(c, _):
        piece = rows_of(c, PIECE)
        part_l[:, piece] = (
            lax.dot_general(hid[...], down[:, piece], TN, preferred_element_type=F32) * HIDDEN_SCALE
        ).astype(BF)
        return 0

    lax.fori_loop(0, PIECES, layer_piece, 0)

    rest_arrived(1)
    own_loads[1].wait()
    pass_on(0, 2)

    dhid[...] = lax.dot_general(down[...], grads[...], NT, preferred_element_type=F32) * HIDDEN_SCALE

    def make_d(i, _):
        r = rows_of(i, 16)
        ru = pl.ds(pl.multiple_of(F + i * 16, 16), 16)
        g = pre[r, :]
        u = pre[ru, :]
        s = jax.nn.sigmoid(g)
        d = dhid[r, :]
        dd[r, :] = (d * u * (s * (1.0 + g * (1.0 - s)))).astype(BF)
        dd[ru, :] = (d * (g * s)).astype(BF)
        return 0

    lax.fori_loop(0, F // 16, make_d, 0)

    def step_wide(c):
        piece = rows_of(c, WCHUNK)
        g = dot(dd[...], acts[:, piece])
        st_wide[:, piece] = (wide[:, piece].astype(F32) - (LEARN_RATE * WIDTH_SCALE) * g).astype(BF)

    def step_send(c, _):
        step_wide(c)
        ex_copy(c).start()
        return 0

    for c in range(long_wide):
        step_wide(c)
        hop(1, c, 0).start()
    lax.fori_loop(long_wide, WCHUNKS, step_send, 0)

    sums = ((part_l, ry_l, sz_l, rz_l, layer_out), (part_g, ry_g, sz_g, rz_g, gradin_out))

    def ry_copy(a, k):
        part, ry = sums[a][:2]
        return send(part.at[rows_of(lax.rem(y + k, 4), 64)], ry.at[k - 1],
                    ry_send.at[a, k - 1], ry_recv.at[a, k - 1], y_peer(k))

    def rz_copy(a, k):
        sz, rz = sums[a][2:4]
        return send(sz.at[rows_of(lax.rem(zh + k, 4), ROWS)], rz.at[k - 1],
                    rz_send.at[a, k - 1], rz_recv.at[a, k - 1], z_peer(k))

    for k in order:
        ry_copy(0, k).start()

    def gradin_piece(c, _):
        piece = rows_of(c, PIECE)
        part_g[:, piece] = (
            lax.dot_general(dd[...], wide[:, piece], TN, preferred_element_type=F32) * WIDTH_SCALE
        ).astype(BF)
        return 0

    lax.fori_loop(0, PIECES, gradin_piece, 0)
    for k in order:
        ry_copy(1, k).start()

    z_forward(2)

    def step_of(w, h, g, piece):
        return (w[:, piece].astype(F32) - (LEARN_RATE * HIDDEN_SCALE) * dot(h[...], g[:, piece])).astype(BF)

    def step_down(c, _):
        piece = rows_of(c, CHUNK)
        st_down[:, piece] = step_of(down, hid, grads, piece)
        return 0

    lax.fori_loop(0, CHUNKS, step_down, 0)
    pass_on(1, 1)

    for a in (0, 1):
        part, ry, sz = sums[a][:3]
        for k in order:
            ry_copy(a, k).wait_recv()

        def sum_y(i, _):
            r = rows_of(i, 16)
            mine = part[rows_of(y * 4 + i, 16), :].astype(F32)
            sz[r, :] = (
                (mine + ry[0, r, :].astype(F32)) + (ry[1, r, :].astype(F32) + ry[2, r, :].astype(F32))
            ).astype(BF)
            return 0

        lax.fori_loop(0, 4, sum_y, 0)
        for k in order:
            rz_copy(a, k).start()

    rest_arrived(2)
    hid_copy.wait_recv()

    def down_write(c):
        piece = rows_of(c, CHUNK)
        return pltpu.make_async_copy(rc_down.at[:, piece], down_out.at[:, piece], down_sem.at[c])

    def average_down(c, _):
        piece = rows_of(c, CHUNK)
        raw_copy(c).wait_recv()
        theirs = step_of(rc_down, phid, pgrads, piece).astype(F32)
        rc_down[:, piece] = ((st_down[:, piece].astype(F32) + theirs) * 0.5).astype(BF)
        down_write(c).start()
        return 0

    lax.fori_loop(0, CHUNKS, average_down, 0)
    pass_on(1, 2)

    def sum_write(a):
        return pltpu.make_async_copy(sums[a][2].at[rows_of(zh, ROWS)], sums[a][4], load_sem.at[3 + a])

    for a in (0, 1):
        sz, rz = sums[a][2:4]
        for k in order:
            rz_copy(a, k).wait_recv()
        total = sz[rows_of(zh, ROWS), :].astype(F32)
        for k in (0, 1, 2):
            total += rz[k].astype(F32)
        sz[rows_of(zh, ROWS), :] = total.astype(BF)
        sum_write(a).start()

    def wide_write(h, c):
        piece = rows_of(c, WCHUNK)
        return pltpu.make_async_copy(
            rc_wide.at[pl.ds(h * F, F), piece], (gate_out, up_out)[h].at[:, piece], wide_sem.at[h, c])

    def average_wide(c, _):
        piece = rows_of(c, WCHUNK)
        ex_copy(c).wait_recv()
        rc_wide[:, piece] = ((st_wide[:, piece].astype(F32) + rc_wide[:, piece].astype(F32)) * 0.5).astype(BF)
        wide_write(0, c).start()
        wide_write(1, c).start()
        return 0

    lax.fori_loop(long_wide, WCHUNKS, average_wide, 0)
    lax.fori_loop(0, long_wide, average_wide, 0)

    for a in (0, 1, 2):
        for k in order:
            z_copy(a, k).wait_send()
            for j in (0, 1, 2, 3):
                y_copy(a, j, k).wait_send()
    for a in (0, 1):
        for k in order:
            ry_copy(a, k).wait_send()
            rz_copy(a, k).wait_send()
        sum_write(a).wait()
    shard_copy.wait_send()
    hid_copy.wait_send()
    for kind in (0, 1):
        for c in range((long_raw, long_wide)[kind]):
            hop(kind, c, 1).wait_send()
            hop(kind, c, 2).wait_send()

    def finish_down(c, _):
        raw_copy(c).wait_send()
        down_write(c).wait()
        return 0

    def finish_wide(c, _):
        ex_copy(c).wait_send()
        wide_write(0, c).wait()
        wide_write(1, c).wait()
        return 0

    lax.fori_loop(0, CHUNKS, finish_down, 0)
    lax.fori_loop(0, WCHUNKS, finish_wide, 0)


def step(level, acts, grads, gate_w, up_w, down_w):
    any_spec = pl.BlockSpec(memory_space=pl.ANY)
    vm = pltpu.VMEM
    dma = pltpu.SemaphoreType.DMA
    tall, stack, full, hidden = (F, D), (2 * F, D), (TOK, D), (F, TOK)
    relay = []
    if level == 2:
        raw_relay, wide_relay = (LONG_RAW, F, CHUNK), (LONG_WIDE, 2 * F, WCHUNK)
        relay = [vm(raw_relay, BF), vm(raw_relay, BF), vm(wide_relay, BF), vm(wide_relay, BF)]
        relay += [dma((2, LONG_RAW + LONG_WIDE)), dma((2, LONG_RAW + LONG_WIDE))]
    return pl.pallas_call(
        partial(kernel, 1 << level),
        out_shape=(
            jax.ShapeDtypeStruct((ROWS, D), BF),
            jax.ShapeDtypeStruct((ROWS, D), BF),
            jax.ShapeDtypeStruct(tall, BF),
            jax.ShapeDtypeStruct(tall, BF),
            jax.ShapeDtypeStruct(tall, BF),
        ),
        in_specs=[any_spec] * 5,
        out_specs=(any_spec,) * 5,
        scratch_shapes=[
            vm(full, BF), vm(full, BF), vm(full, BF), vm(stack, BF), vm(tall, BF),
            vm(stack, BF), vm(tall, BF), vm(stack, BF), vm(tall, BF),
            vm((2 * F, TOK), F32), vm(hidden, F32), vm(hidden, BF), vm(hidden, BF), vm((2 * F, TOK), BF),
            vm(full, BF), vm(full, BF),
            vm((3, 64, D), BF), vm((3, 64, D), BF), vm((64, D), BF), vm((64, D), BF),
            vm((3, ROWS, D), BF), vm((3, ROWS, D), BF),
            dma((5,)), dma((3, 16)), dma((3, 3)), dma((3, 4, 3)), dma,
            dma((CHUNKS,)), dma((CHUNKS,)), dma, dma, dma((WCHUNKS,)), dma((WCHUNKS,)),
            dma((2, 3)), dma((2, 3)), dma((2, 3)), dma((2, 3)), dma((CHUNKS,)), dma((2, WCHUNKS)),
            *relay,
        ],
        compiler_params=pltpu.CompilerParams(
            collective_id=level, has_side_effects=True, vmem_limit_bytes=KERNEL_VMEM),
        name=f"gossip_step_{1 << level}",
    )(acts, grads, gate_w, up_w, down_w)


def emit_kernel(*refs):
    sources, targets, (hold, in_sem, out_sem) = refs[:5], refs[5:10], refs[10:]
    small = [pltpu.make_async_copy(sources[i], targets[i], out_sem.at[i]) for i in (0, 1)]
    reads, writes = [], []
    for i in range(2, 5):
        for part in range(EMIT_PARTS):
            n = (i - 2) * EMIT_PARTS + part
            rows = pl.ds(part * EMIT_ROWS, EMIT_ROWS)
            reads.append(pltpu.make_async_copy(sources[i].at[rows], hold.at[n], in_sem.at[n]))
            writes.append(pltpu.make_async_copy(hold.at[n], targets[i].at[rows], out_sem.at[2 + n]))
    for copy in small + reads:
        copy.start()
    for read, write in zip(reads, writes):
        read.wait()
        write.start()
    for copy in small + writes:
        copy.wait()


def emit(arrays):
    any_spec = pl.BlockSpec(memory_space=pl.ANY)
    parts = 3 * EMIT_PARTS
    return pl.pallas_call(
        emit_kernel,
        out_shape=tuple(jax.ShapeDtypeStruct(a.shape, a.dtype) for a in arrays),
        in_specs=[any_spec] * 5,
        out_specs=(any_spec,) * 5,
        scratch_shapes=[
            pltpu.VMEM((parts, EMIT_ROWS, D), BF),
            pltpu.SemaphoreType.DMA((parts,)), pltpu.SemaphoreType.DMA((2 + parts,)),
        ],
        compiler_params=pltpu.CompilerParams(vmem_limit_bytes=12 * 1024 * 1024),
        name="emit",
    )(*arrays)


def shards(activations, out_grad, gate_weight, up_weight, down_weight, step_index):
    level = step_index[0] % 4
    outs = lax.switch(
        level,
        [partial(step, i) for i in range(4)],
        activations[0], out_grad[0], gate_weight[0].T, up_weight[0].T, down_weight[0],
    )
    outs = emit(outs)
    return outs[0][None], outs[1][None], outs[2].T[None], outs[3].T[None], outs[4][None]


def solution(mesh):
    in_specs = (
        P("rep", "tp", None),
        P("rep", "tp", None),
        P("rep", None, "tp"),
        P("rep", None, "tp"),
        P("rep", "tp", None),
        P(),
    )
    out_specs = (
        P("rep", "tp", None),
        P("rep", "tp", None),
        P("rep", None, "tp"),
        P("rep", None, "tp"),
        P("rep", "tp", None),
    )
    return jax.shard_map(shards, mesh=mesh, in_specs=in_specs, out_specs=out_specs, check_vma=False)
```

```python
from functools import partial
import math

import jax
import jax.numpy as jnp
from jax import lax
from jax.experimental import pallas as pl
from jax.experimental.pallas import tpu as pltpu
from jax.sharding import PartitionSpec as P

D = 2560
FF = 6912
TOK = 256
TP = 16
F = FF // TP
ROWS = TOK // TP

LEARN_RATE = 0.8
WIDTH_SCALE = 1.0 / math.sqrt(D)
HIDDEN_SCALE = 1.0 / math.sqrt(FF)

CHUNK = 256
CHUNKS = D // CHUNK
PIECE = 512
PIECES = D // PIECE
WCHUNK = 256
WCHUNKS = D // WCHUNK
LONG_RAW = 3
LONG_WIDE = 2
FIRST = {1: (5, 6), 2: (4, 4), 4: (CHUNKS, WCHUNKS), 8: (CHUNKS, WCHUNKS)}

KERNEL_VMEM = 56 * 1024 * 1024
EMIT_PARTS = 3
EMIT_ROWS = F // EMIT_PARTS

MESH = pl.DeviceIdType.MESH
BF = jnp.bfloat16
F32 = jnp.float32

NT = (((1,), (1,)), ((), ()))
TN = (((0,), (0,)), ((), ()))


def rows_of(block, size):
    return pl.ds(pl.multiple_of(block * size, size), size)


def dot(a, b):
    return jnp.dot(a, b, preferred_element_type=F32)


def kernel(
    dist,
    acts_in, grads_in, gate_in, up_in, down_in,
    layer_out, gradin_out, gate_out, up_out, down_out,
    acts, grads, pgrads, wide, down,
    st_wide, st_down, rc_wide, rc_down,
    pre, dhid, hid, phid, dd,
    part_l, part_g, ry_l, ry_g, sz_l, sz_g, rz_l, rz_g,
    load_sem, ag_recv, agz_send, agy_send, shard_send,
    raw_send, raw_recv, hid_send, hid_recv, ex_send, ex_recv,
    ry_send, ry_recv, rz_send, rz_recv, down_sem, wide_sem,
    *relay,
):
    rep = lax.axis_index("rep")
    tp = lax.axis_index("tp")
    zh, y = tp // 4, lax.rem(tp, 4)
    order = (1, 3, 2)

    def z_peer(k):
        return (rep, lax.rem(zh + k, 4) * 4 + y)

    def y_peer(k):
        return (rep, zh * 4 + lax.rem(y + k, 4))

    to_partner = (lax.rem(rep + dist, 16), tp)
    from_partner = (lax.rem(rep + 16 - dist, 16), tp)

    def send(src, dst, send_sem, recv_sem, device):
        return pltpu.make_async_remote_copy(
            src, dst, send_sem, recv_sem, device_id=device, device_id_type=MESH)

    loads = [
        pltpu.make_async_copy(gate_in, wide.at[pl.ds(0, F)], load_sem.at[0]),
        pltpu.make_async_copy(up_in, wide.at[pl.ds(F, F)], load_sem.at[1]),
        pltpu.make_async_copy(down_in, down, load_sem.at[2]),
    ]
    own_block = y * 4 + zh
    own = rows_of(own_block, ROWS)
    own_loads = [
        pltpu.make_async_copy(acts_in, acts.at[own], load_sem.at[3]),
        pltpu.make_async_copy(grads_in, grads.at[own], load_sem.at[4]),
    ]

    barrier = pltpu.get_barrier_semaphore()
    friends = [z_peer(k) for k in (1, 2, 3)] + [y_peer(k) for k in (1, 2, 3)] + [to_partner]
    if dist != 8:
        friends.append(from_partner)
    for friend in friends:
        pl.semaphore_signal(barrier, inc=1, device_id=friend, device_id_type=MESH)
    for copy in own_loads + loads:
        copy.start()
    pl.semaphore_wait(barrier, len(friends))

    sources = ((acts_in, acts), (grads_in, grads), (pgrads.at[own], pgrads))

    def z_copy(a, k):
        src, dst = sources[a]
        return send(src, dst.at[own], agz_send.at[a, k - 1], ag_recv.at[a, own_block], z_peer(k))

    def y_copy(a, j, k):
        src, dst = sources[a]
        b = y * 4 + lax.rem(zh + 4 - j, 4)
        rows = dst.at[rows_of(b, ROWS)]
        return send(src if j == 0 else rows, rows, agy_send.at[a, j, k - 1], ag_recv.at[a, b], y_peer(k))

    def arrived(a, b):
        src, dst = sources[a]
        send(dst.at[rows_of(b, ROWS)], dst.at[rows_of(b, ROWS)], agz_send.at[a, 0], ag_recv.at[a, b],
             z_peer(1)).wait_recv()

    def z_start(a):
        for k in order:
            z_copy(a, k).start()

    def y_start(a, j):
        for k in order:
            y_copy(a, j, k).start()

    def z_forward(a):
        for j in order:
            arrived(a, y * 4 + lax.rem(zh + 4 - j, 4))
            y_start(a, j)

    def rest_arrived(a):
        for k in order:
            for j in (0,) + order:
                arrived(a, lax.rem(y + 4 - k, 4) * 4 + lax.rem(zh + 4 - j, 4))

    shard_copy = send(grads_in, pgrads.at[own], shard_send, ag_recv.at[2, own_block], to_partner)
    hid_copy = send(hid, phid, hid_send, hid_recv, to_partner)

    def raw_copy(c):
        piece = rows_of(c, CHUNK)
        return send(down_in.at[:, piece], rc_down.at[:, piece], raw_send.at[c], raw_recv.at[c], to_partner)

    def ex_copy(c):
        piece = rows_of(c, WCHUNK)
        return send(st_wide.at[:, piece], rc_wide.at[:, piece], ex_send.at[c], ex_recv.at[c], to_partner)

    long_raw, long_wide = (LONG_RAW, LONG_WIDE) if dist == 4 else (0, 0)

    def hop(kind, c, n):
        piece = rows_of(c, CHUNK if kind == 0 else WCHUNK)
        raw_a, raw_b, wide_a, wide_b, relay_send, relay_recv = relay
        i = c if kind == 0 else LONG_RAW + c
        a, b = (raw_a.at[c], raw_b.at[c]) if kind == 0 else (wide_a.at[c], wide_b.at[c])
        src, dst = ((down_in, rc_down), (st_wide, rc_wide))[kind]
        first_send, last_recv = ((raw_send, raw_recv), (ex_send, ex_recv))[kind]
        if n == 0:
            return send(src.at[:, piece], a, first_send.at[c], relay_recv.at[0, i], from_partner)
        if n == 1:
            return send(a, b, relay_send.at[0, i], relay_recv.at[1, i], from_partner)
        return send(b, dst.at[:, piece], relay_send.at[1, i], last_recv.at[c], from_partner)

    def pass_on(kind, n):
        for c in range((long_raw, long_wide)[kind]):
            hop(kind, c, n - 1).wait_recv()
            hop(kind, c, n).start()

    first_raw, first_wide = FIRST[dist]

    def start_raw():
        for c in range(long_raw):
            hop(0, c, 0).start()

        lax.fori_loop(long_raw, first_raw, start_one(raw_copy), 0)

    def start_one(copy):
        def one(c, _):
            copy(c).start()
            return 0
        return one

    z_start(0)
    y_start(0, 0)
    z_start(1)
    y_start(1, 0)
    shard_copy.start()
    start_raw()
    z_forward(0)
    z_forward(1)
    arrived(2, own_block)
    z_start(2)
    lax.fori_loop(first_raw, CHUNKS, start_one(raw_copy), 0)
    y_start(2, 0)
    pass_on(0, 1)

    rest_arrived(0)
    own_loads[0].wait()
    loads[0].wait()
    loads[1].wait()
    pre[...] = lax.dot_general(wide[...], acts[...], NT, preferred_element_type=F32) * WIDTH_SCALE

    def make_hidden(i, _):
        r = rows_of(i, 16)
        g = pre[r, :]
        u = pre[pl.ds(pl.multiple_of(F + i * 16, 16), 16), :]
        hid[r, :] = (g * jax.nn.sigmoid(g) * u).astype(BF)
        return 0

    lax.fori_loop(0, F // 16, make_hidden, 0)
    hid_copy.start()

    loads[2].wait()

    def layer_piece(c, _):
        piece = rows_of(c, PIECE)
        part_l[:, piece] = (
            lax.dot_general(hid[...], down[:, piece], TN, preferred_element_type=F32) * HIDDEN_SCALE
        ).astype(BF)
        return 0

    lax.fori_loop(0, PIECES, layer_piece, 0)

    rest_arrived(1)
    own_loads[1].wait()
    pass_on(0, 2)

    dhid[...] = lax.dot_general(down[...], grads[...], NT, preferred_element_type=F32) * HIDDEN_SCALE

    def make_d(i, _):
        r = rows_of(i, 16)
        ru = pl.ds(pl.multiple_of(F + i * 16, 16), 16)
        g = pre[r, :]
        u = pre[ru, :]
        s = jax.nn.sigmoid(g)
        d = dhid[r, :]
        dd[r, :] = (d * u * (s * (1.0 + g * (1.0 - s)))).astype(BF)
        dd[ru, :] = (d * (g * s)).astype(BF)
        return 0

    lax.fori_loop(0, F // 16, make_d, 0)

    def step_wide(c):
        piece = rows_of(c, WCHUNK)
        g = dot(dd[...], acts[:, piece])
        st_wide[:, piece] = (wide[:, piece].astype(F32) - (LEARN_RATE * WIDTH_SCALE) * g).astype(BF)

    def step_send(c, _):
        step_wide(c)
        ex_copy(c).start()
        return 0

    def step_only(c, _):
        step_wide(c)
        return 0

    for c in range(long_wide):
        step_wide(c)
        hop(1, c, 0).start()
    lax.fori_loop(long_wide, first_wide, step_send, 0)
    lax.fori_loop(first_wide, WCHUNKS, step_only, 0)

    sums = ((part_l, ry_l, sz_l, rz_l, layer_out), (part_g, ry_g, sz_g, rz_g, gradin_out))

    def ry_copy(a, k):
        part, ry = sums[a][:2]
        return send(part.at[rows_of(lax.rem(y + k, 4), 64)], ry.at[k - 1],
                    ry_send.at[a, k - 1], ry_recv.at[a, k - 1], y_peer(k))

    def rz_copy(a, k):
        sz, rz = sums[a][2:4]
        return send(sz.at[rows_of(lax.rem(zh + k, 4), ROWS)], rz.at[k - 1],
                    rz_send.at[a, k - 1], rz_recv.at[a, k - 1], z_peer(k))

    for k in order:
        ry_copy(0, k).start()

    def gradin_piece(c, _):
        piece = rows_of(c, PIECE)
        part_g[:, piece] = (
            lax.dot_general(dd[...], wide[:, piece], TN, preferred_element_type=F32) * WIDTH_SCALE
        ).astype(BF)
        return 0

    lax.fori_loop(0, PIECES, gradin_piece, 0)
    for k in order:
        ry_copy(1, k).start()

    z_forward(2)

    def step_of(w, h, g, piece):
        return (w[:, piece].astype(F32) - (LEARN_RATE * HIDDEN_SCALE) * dot(h[...], g[:, piece])).astype(BF)

    def step_down(c, _):
        piece = rows_of(c, CHUNK)
        st_down[:, piece] = step_of(down, hid, grads, piece)
        return 0

    lax.fori_loop(0, CHUNKS, step_down, 0)
    pass_on(1, 1)

    for a in (0, 1):
        part, ry, sz = sums[a][:3]
        for k in order:
            ry_copy(a, k).wait_recv()

        def sum_y(i, _):
            r = rows_of(i, 16)
            mine = part[rows_of(y * 4 + i, 16), :].astype(F32)
            sz[r, :] = (
                (mine + ry[0, r, :].astype(F32)) + (ry[1, r, :].astype(F32) + ry[2, r, :].astype(F32))
            ).astype(BF)
            return 0

        lax.fori_loop(0, 4, sum_y, 0)
        for k in order:
            rz_copy(a, k).start()

    lax.fori_loop(first_wide, WCHUNKS, start_one(ex_copy), 0)

    pass_on(1, 2)
    rest_arrived(2)
    hid_copy.wait_recv()

    def down_write(c):
        piece = rows_of(c, CHUNK)
        return pltpu.make_async_copy(rc_down.at[:, piece], down_out.at[:, piece], down_sem.at[c])

    def average_down(c, _):
        piece = rows_of(c, CHUNK)
        raw_copy(c).wait_recv()
        theirs = step_of(rc_down, phid, pgrads, piece).astype(F32)
        rc_down[:, piece] = ((st_down[:, piece].astype(F32) + theirs) * 0.5).astype(BF)
        down_write(c).start()
        return 0

    lax.fori_loop(0, CHUNKS, average_down, 0)

    def sum_write(a):
        return pltpu.make_async_copy(sums[a][2].at[rows_of(zh, ROWS)], sums[a][4], load_sem.at[3 + a])

    for a in (0, 1):
        sz, rz = sums[a][2:4]
        for k in order:
            rz_copy(a, k).wait_recv()
        total = sz[rows_of(zh, ROWS), :].astype(F32)
        for k in (0, 1, 2):
            total += rz[k].astype(F32)
        sz[rows_of(zh, ROWS), :] = total.astype(BF)
        sum_write(a).start()

    def wide_write(h, c):
        piece = rows_of(c, WCHUNK)
        return pltpu.make_async_copy(
            rc_wide.at[pl.ds(h * F, F), piece], (gate_out, up_out)[h].at[:, piece], wide_sem.at[h, c])

    def average_wide(c, _):
        piece = rows_of(c, WCHUNK)
        ex_copy(c).wait_recv()
        rc_wide[:, piece] = ((st_wide[:, piece].astype(F32) + rc_wide[:, piece].astype(F32)) * 0.5).astype(BF)
        wide_write(0, c).start()
        wide_write(1, c).start()
        return 0

    lax.fori_loop(long_wide, WCHUNKS, average_wide, 0)
    lax.fori_loop(0, long_wide, average_wide, 0)

    for a in (0, 1, 2):
        for k in order:
            z_copy(a, k).wait_send()
            for j in (0, 1, 2, 3):
                y_copy(a, j, k).wait_send()
    for a in (0, 1):
        for k in order:
            ry_copy(a, k).wait_send()
            rz_copy(a, k).wait_send()
        sum_write(a).wait()
    shard_copy.wait_send()
    hid_copy.wait_send()
    for kind in (0, 1):
        for c in range((long_raw, long_wide)[kind]):
            hop(kind, c, 1).wait_send()
            hop(kind, c, 2).wait_send()

    def finish_down(c, _):
        raw_copy(c).wait_send()
        down_write(c).wait()
        return 0

    def finish_wide(c, _):
        ex_copy(c).wait_send()
        wide_write(0, c).wait()
        wide_write(1, c).wait()
        return 0

    lax.fori_loop(0, CHUNKS, finish_down, 0)
    lax.fori_loop(0, WCHUNKS, finish_wide, 0)


def step(level, acts, grads, gate_w, up_w, down_w):
    any_spec = pl.BlockSpec(memory_space=pl.ANY)
    vm = pltpu.VMEM
    dma = pltpu.SemaphoreType.DMA
    tall, stack, full, hidden = (F, D), (2 * F, D), (TOK, D), (F, TOK)
    relay = []
    if level == 2:
        raw_relay, wide_relay = (LONG_RAW, F, CHUNK), (LONG_WIDE, 2 * F, WCHUNK)
        relay = [vm(raw_relay, BF), vm(raw_relay, BF), vm(wide_relay, BF), vm(wide_relay, BF)]
        relay += [dma((2, LONG_RAW + LONG_WIDE)), dma((2, LONG_RAW + LONG_WIDE))]
    return pl.pallas_call(
        partial(kernel, 1 << level),
        out_shape=(
            jax.ShapeDtypeStruct((ROWS, D), BF),
            jax.ShapeDtypeStruct((ROWS, D), BF),
            jax.ShapeDtypeStruct(tall, BF),
            jax.ShapeDtypeStruct(tall, BF),
            jax.ShapeDtypeStruct(tall, BF),
        ),
        in_specs=[any_spec] * 5,
        out_specs=(any_spec,) * 5,
        scratch_shapes=[
            vm(full, BF), vm(full, BF), vm(full, BF), vm(stack, BF), vm(tall, BF),
            vm(stack, BF), vm(tall, BF), vm(stack, BF), vm(tall, BF),
            vm((2 * F, TOK), F32), vm(hidden, F32), vm(hidden, BF), vm(hidden, BF), vm((2 * F, TOK), BF),
            vm(full, BF), vm(full, BF),
            vm((3, 64, D), BF), vm((3, 64, D), BF), vm((64, D), BF), vm((64, D), BF),
            vm((3, ROWS, D), BF), vm((3, ROWS, D), BF),
            dma((5,)), dma((3, 16)), dma((3, 3)), dma((3, 4, 3)), dma,
            dma((CHUNKS,)), dma((CHUNKS,)), dma, dma, dma((WCHUNKS,)), dma((WCHUNKS,)),
            dma((2, 3)), dma((2, 3)), dma((2, 3)), dma((2, 3)), dma((CHUNKS,)), dma((2, WCHUNKS)),
            *relay,
        ],
        compiler_params=pltpu.CompilerParams(
            collective_id=level, has_side_effects=True, vmem_limit_bytes=KERNEL_VMEM),
        name=f"gossip_step_{1 << level}",
    )(acts, grads, gate_w, up_w, down_w)


def emit_kernel(*refs):
    sources, targets, (hold, in_sem, out_sem) = refs[:5], refs[5:10], refs[10:]
    small = [pltpu.make_async_copy(sources[i], targets[i], out_sem.at[i]) for i in (0, 1)]
    reads, writes = [], []
    for i in range(2, 5):
        for part in range(EMIT_PARTS):
            n = (i - 2) * EMIT_PARTS + part
            rows = pl.ds(part * EMIT_ROWS, EMIT_ROWS)
            reads.append(pltpu.make_async_copy(sources[i].at[rows], hold.at[n], in_sem.at[n]))
            writes.append(pltpu.make_async_copy(hold.at[n], targets[i].at[rows], out_sem.at[2 + n]))
    for copy in small + reads:
        copy.start()
    for read, write in zip(reads, writes):
        read.wait()
        write.start()
    for copy in small + writes:
        copy.wait()


def emit(arrays):
    any_spec = pl.BlockSpec(memory_space=pl.ANY)
    parts = 3 * EMIT_PARTS
    return pl.pallas_call(
        emit_kernel,
        out_shape=tuple(jax.ShapeDtypeStruct(a.shape, a.dtype) for a in arrays),
        in_specs=[any_spec] * 5,
        out_specs=(any_spec,) * 5,
        scratch_shapes=[
            pltpu.VMEM((parts, EMIT_ROWS, D), BF),
            pltpu.SemaphoreType.DMA((parts,)), pltpu.SemaphoreType.DMA((2 + parts,)),
        ],
        compiler_params=pltpu.CompilerParams(vmem_limit_bytes=12 * 1024 * 1024),
        name="emit",
    )(*arrays)


def shards(activations, out_grad, gate_weight, up_weight, down_weight, step_index):
    level = step_index[0] % 4
    outs = lax.switch(
        level,
        [partial(step, i) for i in range(4)],
        activations[0], out_grad[0], gate_weight[0].T, up_weight[0].T, down_weight[0],
    )
    outs = emit(outs)
    return outs[0][None], outs[1][None], outs[2].T[None], outs[3].T[None], outs[4][None]


def solution(mesh):
    in_specs = (
        P("rep", "tp", None),
        P("rep", "tp", None),
        P("rep", None, "tp"),
        P("rep", None, "tp"),
        P("rep", "tp", None),
        P(),
    )
    out_specs = (
        P("rep", "tp", None),
        P("rep", "tp", None),
        P("rep", None, "tp"),
        P("rep", None, "tp"),
        P("rep", "tp", None),
    )
    return jax.shard_map(shards, mesh=mesh, in_specs=in_specs, out_specs=out_specs, check_vma=False)
```

```python
from functools import partial
import math

import jax
import jax.numpy as jnp
from jax import lax
from jax.experimental import pallas as pl
from jax.experimental.pallas import tpu as pltpu
from jax.sharding import PartitionSpec as P

D = 2560
FF = 6912
TOK = 256
TP = 16
F = FF // TP
ROWS = TOK // TP

LEARN_RATE = 0.8
WIDTH_SCALE = 1.0 / math.sqrt(D)
HIDDEN_SCALE = 1.0 / math.sqrt(FF)

CHUNK = 256
CHUNKS = D // CHUNK
PIECE = 512
PIECES = D // PIECE
WCHUNK = 256
WCHUNKS = D // WCHUNK
LONG_RAW = 3
LONG_WIDE = 2
FIRST = {1: (5, 6), 2: (4, 4), 4: (CHUNKS, WCHUNKS), 8: (CHUNKS, WCHUNKS)}

KERNEL_VMEM = 56 * 1024 * 1024
EMIT_PARTS = 9
EMIT_ROWS = F // EMIT_PARTS

MESH = pl.DeviceIdType.MESH
BF = jnp.bfloat16
F32 = jnp.float32

NT = (((1,), (1,)), ((), ()))
TN = (((0,), (0,)), ((), ()))


def rows_of(block, size):
    return pl.ds(pl.multiple_of(block * size, size), size)


def dot(a, b):
    return jnp.dot(a, b, preferred_element_type=F32)


def kernel(
    dist,
    acts_in, grads_in, gate_in, up_in, down_in,
    layer_out, gradin_out, gate_out, up_out, down_out,
    acts, grads, pgrads, wide, down,
    st_wide, st_down, rc_wide, rc_down,
    pre, dhid, hid, phid, dd,
    part_l, part_g, ry_l, ry_g, sz_l, sz_g, rz_l, rz_g,
    load_sem, ag_recv, agz_send, agy_send, shard_send,
    raw_send, raw_recv, hid_send, hid_recv, ex_send, ex_recv,
    ry_send, ry_recv, rz_send, rz_recv, down_sem, wide_sem,
    *relay,
):
    rep = lax.axis_index("rep")
    tp = lax.axis_index("tp")
    zh, y = tp // 4, lax.rem(tp, 4)
    order = (1, 3, 2)

    def z_peer(k):
        return (rep, lax.rem(zh + k, 4) * 4 + y)

    def y_peer(k):
        return (rep, zh * 4 + lax.rem(y + k, 4))

    to_partner = (lax.rem(rep + dist, 16), tp)
    from_partner = (lax.rem(rep + 16 - dist, 16), tp)

    def send(src, dst, send_sem, recv_sem, device):
        return pltpu.make_async_remote_copy(
            src, dst, send_sem, recv_sem, device_id=device, device_id_type=MESH)

    loads = [
        pltpu.make_async_copy(gate_in, wide.at[pl.ds(0, F)], load_sem.at[0]),
        pltpu.make_async_copy(up_in, wide.at[pl.ds(F, F)], load_sem.at[1]),
        pltpu.make_async_copy(down_in, down, load_sem.at[2]),
    ]
    own_block = y * 4 + zh
    own = rows_of(own_block, ROWS)
    own_loads = [
        pltpu.make_async_copy(acts_in, acts.at[own], load_sem.at[3]),
        pltpu.make_async_copy(grads_in, grads.at[own], load_sem.at[4]),
    ]

    barrier = pltpu.get_barrier_semaphore()
    friends = [z_peer(k) for k in (1, 2, 3)] + [y_peer(k) for k in (1, 2, 3)] + [to_partner]
    if dist != 8:
        friends.append(from_partner)
    for friend in friends:
        pl.semaphore_signal(barrier, inc=1, device_id=friend, device_id_type=MESH)
    for copy in own_loads + loads:
        copy.start()
    pl.semaphore_wait(barrier, len(friends))

    sources = ((acts_in, acts), (grads_in, grads), (pgrads.at[own], pgrads))

    def z_copy(a, k):
        src, dst = sources[a]
        return send(src, dst.at[own], agz_send.at[a, k - 1], ag_recv.at[a, own_block], z_peer(k))

    def y_copy(a, j, k):
        src, dst = sources[a]
        b = y * 4 + lax.rem(zh + 4 - j, 4)
        rows = dst.at[rows_of(b, ROWS)]
        return send(src if j == 0 else rows, rows, agy_send.at[a, j, k - 1], ag_recv.at[a, b], y_peer(k))

    def arrived(a, b):
        src, dst = sources[a]
        send(dst.at[rows_of(b, ROWS)], dst.at[rows_of(b, ROWS)], agz_send.at[a, 0], ag_recv.at[a, b],
             z_peer(1)).wait_recv()

    def z_start(a):
        for k in order:
            z_copy(a, k).start()

    def y_start(a, j):
        for k in order:
            y_copy(a, j, k).start()

    def z_forward(a):
        for j in order:
            arrived(a, y * 4 + lax.rem(zh + 4 - j, 4))
            y_start(a, j)

    def rest_arrived(a):
        for k in order:
            for j in (0,) + order:
                arrived(a, lax.rem(y + 4 - k, 4) * 4 + lax.rem(zh + 4 - j, 4))

    shard_copy = send(grads_in, pgrads.at[own], shard_send, ag_recv.at[2, own_block], to_partner)
    hid_copy = send(hid, phid, hid_send, hid_recv, to_partner)

    def raw_copy(c):
        piece = rows_of(c, CHUNK)
        return send(down_in.at[:, piece], rc_down.at[:, piece], raw_send.at[c], raw_recv.at[c], to_partner)

    def ex_copy(c):
        piece = rows_of(c, WCHUNK)
        return send(st_wide.at[:, piece], rc_wide.at[:, piece], ex_send.at[c], ex_recv.at[c], to_partner)

    long_raw, long_wide = (LONG_RAW, LONG_WIDE) if dist == 4 else (0, 0)

    def hop(kind, c, n):
        piece = rows_of(c, CHUNK if kind == 0 else WCHUNK)
        raw_a, raw_b, wide_a, wide_b, relay_send, relay_recv = relay
        i = c if kind == 0 else LONG_RAW + c
        a, b = (raw_a.at[c], raw_b.at[c]) if kind == 0 else (wide_a.at[c], wide_b.at[c])
        src, dst = ((down_in, rc_down), (st_wide, rc_wide))[kind]
        first_send, last_recv = ((raw_send, raw_recv), (ex_send, ex_recv))[kind]
        if n == 0:
            return send(src.at[:, piece], a, first_send.at[c], relay_recv.at[0, i], from_partner)
        if n == 1:
            return send(a, b, relay_send.at[0, i], relay_recv.at[1, i], from_partner)
        return send(b, dst.at[:, piece], relay_send.at[1, i], last_recv.at[c], from_partner)

    def pass_on(kind, n):
        for c in range((long_raw, long_wide)[kind]):
            hop(kind, c, n - 1).wait_recv()
            hop(kind, c, n).start()

    first_raw, first_wide = FIRST[dist]

    def start_raw():
        for c in range(long_raw):
            hop(0, c, 0).start()

        lax.fori_loop(long_raw, first_raw, start_one(raw_copy), 0)

    def start_one(copy):
        def one(c, _):
            copy(c).start()
            return 0
        return one

    z_start(0)
    y_start(0, 0)
    z_start(1)
    y_start(1, 0)
    shard_copy.start()
    start_raw()
    z_forward(0)
    z_forward(1)
    arrived(2, own_block)
    z_start(2)
    lax.fori_loop(first_raw, CHUNKS, start_one(raw_copy), 0)
    y_start(2, 0)
    pass_on(0, 1)

    rest_arrived(0)
    own_loads[0].wait()
    loads[0].wait()
    loads[1].wait()
    pre[...] = lax.dot_general(wide[...], acts[...], NT, preferred_element_type=F32) * WIDTH_SCALE

    def make_hidden(i, _):
        r = rows_of(i, 16)
        g = pre[r, :]
        u = pre[pl.ds(pl.multiple_of(F + i * 16, 16), 16), :]
        hid[r, :] = (g * jax.nn.sigmoid(g) * u).astype(BF)
        return 0

    lax.fori_loop(0, F // 16, make_hidden, 0)
    hid_copy.start()

    loads[2].wait()

    def layer_piece(c, _):
        piece = rows_of(c, PIECE)
        part_l[:, piece] = (
            lax.dot_general(hid[...], down[:, piece], TN, preferred_element_type=F32) * HIDDEN_SCALE
        ).astype(BF)
        return 0

    lax.fori_loop(0, PIECES, layer_piece, 0)

    rest_arrived(1)
    own_loads[1].wait()
    pass_on(0, 2)

    dhid[...] = lax.dot_general(down[...], grads[...], NT, preferred_element_type=F32) * HIDDEN_SCALE

    def make_d(i, _):
        r = rows_of(i, 16)
        ru = pl.ds(pl.multiple_of(F + i * 16, 16), 16)
        g = pre[r, :]
        u = pre[ru, :]
        s = jax.nn.sigmoid(g)
        d = dhid[r, :]
        dd[r, :] = (d * u * (s * (1.0 + g * (1.0 - s)))).astype(BF)
        dd[ru, :] = (d * (g * s)).astype(BF)
        return 0

    lax.fori_loop(0, F // 16, make_d, 0)

    def step_wide(c):
        piece = rows_of(c, WCHUNK)
        g = dot(dd[...], acts[:, piece])
        st_wide[:, piece] = (wide[:, piece].astype(F32) - (LEARN_RATE * WIDTH_SCALE) * g).astype(BF)

    def step_send(c, _):
        step_wide(c)
        ex_copy(c).start()
        return 0

    def step_only(c, _):
        step_wide(c)
        return 0

    for c in range(long_wide):
        step_wide(c)
        hop(1, c, 0).start()
    lax.fori_loop(long_wide, first_wide, step_send, 0)
    lax.fori_loop(first_wide, WCHUNKS, step_only, 0)

    sums = ((part_l, ry_l, sz_l, rz_l, layer_out), (part_g, ry_g, sz_g, rz_g, gradin_out))

    def ry_copy(a, k):
        part, ry = sums[a][:2]
        return send(part.at[rows_of(lax.rem(y + k, 4), 64)], ry.at[k - 1],
                    ry_send.at[a, k - 1], ry_recv.at[a, k - 1], y_peer(k))

    def rz_copy(a, k):
        sz, rz = sums[a][2:4]
        return send(sz.at[rows_of(lax.rem(zh + k, 4), ROWS)], rz.at[k - 1],
                    rz_send.at[a, k - 1], rz_recv.at[a, k - 1], z_peer(k))

    for k in order:
        ry_copy(0, k).start()

    def gradin_piece(c, _):
        piece = rows_of(c, PIECE)
        part_g[:, piece] = (
            lax.dot_general(dd[...], wide[:, piece], TN, preferred_element_type=F32) * WIDTH_SCALE
        ).astype(BF)
        return 0

    lax.fori_loop(0, PIECES, gradin_piece, 0)
    for k in order:
        ry_copy(1, k).start()

    z_forward(2)

    def step_of(w, h, g, piece):
        return (w[:, piece].astype(F32) - (LEARN_RATE * HIDDEN_SCALE) * dot(h[...], g[:, piece])).astype(BF)

    def step_down(c, _):
        piece = rows_of(c, CHUNK)
        st_down[:, piece] = step_of(down, hid, grads, piece)
        return 0

    lax.fori_loop(0, CHUNKS, step_down, 0)
    pass_on(1, 1)

    for a in (0, 1):
        part, ry, sz = sums[a][:3]
        for k in order:
            ry_copy(a, k).wait_recv()

        def sum_y(i, _):
            r = rows_of(i, 16)
            mine = part[rows_of(y * 4 + i, 16), :].astype(F32)
            sz[r, :] = (
                (mine + ry[0, r, :].astype(F32)) + (ry[1, r, :].astype(F32) + ry[2, r, :].astype(F32))
            ).astype(BF)
            return 0

        lax.fori_loop(0, 4, sum_y, 0)
        for k in order:
            rz_copy(a, k).start()

    lax.fori_loop(first_wide, WCHUNKS, start_one(ex_copy), 0)

    pass_on(1, 2)
    rest_arrived(2)
    hid_copy.wait_recv()

    def down_write(c):
        piece = rows_of(c, CHUNK)
        return pltpu.make_async_copy(rc_down.at[:, piece], down_out.at[:, piece], down_sem.at[c])

    def average_down(c, _):
        piece = rows_of(c, CHUNK)
        raw_copy(c).wait_recv()
        theirs = step_of(rc_down, phid, pgrads, piece).astype(F32)
        rc_down[:, piece] = ((st_down[:, piece].astype(F32) + theirs) * 0.5).astype(BF)
        down_write(c).start()
        return 0

    lax.fori_loop(0, CHUNKS, average_down, 0)

    def sum_write(a):
        return pltpu.make_async_copy(sums[a][2].at[rows_of(zh, ROWS)], sums[a][4], load_sem.at[3 + a])

    for a in (0, 1):
        sz, rz = sums[a][2:4]
        for k in order:
            rz_copy(a, k).wait_recv()
        total = sz[rows_of(zh, ROWS), :].astype(F32)
        for k in (0, 1, 2):
            total += rz[k].astype(F32)
        sz[rows_of(zh, ROWS), :] = total.astype(BF)
        sum_write(a).start()

    def wide_write(h, c):
        piece = rows_of(c, WCHUNK)
        return pltpu.make_async_copy(
            rc_wide.at[pl.ds(h * F, F), piece], (gate_out, up_out)[h].at[:, piece], wide_sem.at[h, c])

    def average_wide(c, _):
        piece = rows_of(c, WCHUNK)
        ex_copy(c).wait_recv()
        rc_wide[:, piece] = ((st_wide[:, piece].astype(F32) + rc_wide[:, piece].astype(F32)) * 0.5).astype(BF)
        wide_write(0, c).start()
        wide_write(1, c).start()
        return 0

    lax.fori_loop(long_wide, WCHUNKS, average_wide, 0)
    lax.fori_loop(0, long_wide, average_wide, 0)

    for a in (0, 1, 2):
        for k in order:
            z_copy(a, k).wait_send()
            for j in (0, 1, 2, 3):
                y_copy(a, j, k).wait_send()
    for a in (0, 1):
        for k in order:
            ry_copy(a, k).wait_send()
            rz_copy(a, k).wait_send()
        sum_write(a).wait()
    shard_copy.wait_send()
    hid_copy.wait_send()
    for kind in (0, 1):
        for c in range((long_raw, long_wide)[kind]):
            hop(kind, c, 1).wait_send()
            hop(kind, c, 2).wait_send()

    def finish_down(c, _):
        raw_copy(c).wait_send()
        down_write(c).wait()
        return 0

    def finish_wide(c, _):
        ex_copy(c).wait_send()
        wide_write(0, c).wait()
        wide_write(1, c).wait()
        return 0

    lax.fori_loop(0, CHUNKS, finish_down, 0)
    lax.fori_loop(0, WCHUNKS, finish_wide, 0)


def step(level, acts, grads, gate_w, up_w, down_w):
    any_spec = pl.BlockSpec(memory_space=pl.ANY)
    vm = pltpu.VMEM
    dma = pltpu.SemaphoreType.DMA
    tall, stack, full, hidden = (F, D), (2 * F, D), (TOK, D), (F, TOK)
    relay = []
    if level == 2:
        raw_relay, wide_relay = (LONG_RAW, F, CHUNK), (LONG_WIDE, 2 * F, WCHUNK)
        relay = [vm(raw_relay, BF), vm(raw_relay, BF), vm(wide_relay, BF), vm(wide_relay, BF)]
        relay += [dma((2, LONG_RAW + LONG_WIDE)), dma((2, LONG_RAW + LONG_WIDE))]
    return pl.pallas_call(
        partial(kernel, 1 << level),
        out_shape=(
            jax.ShapeDtypeStruct((ROWS, D), BF),
            jax.ShapeDtypeStruct((ROWS, D), BF),
            jax.ShapeDtypeStruct(tall, BF),
            jax.ShapeDtypeStruct(tall, BF),
            jax.ShapeDtypeStruct(tall, BF),
        ),
        in_specs=[any_spec] * 5,
        out_specs=(any_spec,) * 5,
        scratch_shapes=[
            vm(full, BF), vm(full, BF), vm(full, BF), vm(stack, BF), vm(tall, BF),
            vm(stack, BF), vm(tall, BF), vm(stack, BF), vm(tall, BF),
            vm((2 * F, TOK), F32), vm(hidden, F32), vm(hidden, BF), vm(hidden, BF), vm((2 * F, TOK), BF),
            vm(full, BF), vm(full, BF),
            vm((3, 64, D), BF), vm((3, 64, D), BF), vm((64, D), BF), vm((64, D), BF),
            vm((3, ROWS, D), BF), vm((3, ROWS, D), BF),
            dma((5,)), dma((3, 16)), dma((3, 3)), dma((3, 4, 3)), dma,
            dma((CHUNKS,)), dma((CHUNKS,)), dma, dma, dma((WCHUNKS,)), dma((WCHUNKS,)),
            dma((2, 3)), dma((2, 3)), dma((2, 3)), dma((2, 3)), dma((CHUNKS,)), dma((2, WCHUNKS)),
            *relay,
        ],
        compiler_params=pltpu.CompilerParams(
            collective_id=level, has_side_effects=True, vmem_limit_bytes=KERNEL_VMEM),
        name=f"gossip_step_{1 << level}",
    )(acts, grads, gate_w, up_w, down_w)


def emit_kernel(*refs):
    sources, targets, (hold, in_sem, out_sem) = refs[:5], refs[5:10], refs[10:]
    small = [pltpu.make_async_copy(sources[i], targets[i], out_sem.at[i]) for i in (0, 1)]
    reads, writes = [], []
    for i in range(2, 5):
        for part in range(EMIT_PARTS):
            n = (i - 2) * EMIT_PARTS + part
            rows = pl.ds(part * EMIT_ROWS, EMIT_ROWS)
            reads.append(pltpu.make_async_copy(sources[i].at[rows], hold.at[n], in_sem.at[n]))
            writes.append(pltpu.make_async_copy(hold.at[n], targets[i].at[rows], out_sem.at[2 + n]))
    for copy in small + reads:
        copy.start()
    for read, write in zip(reads, writes):
        read.wait()
        write.start()
    for copy in small + writes:
        copy.wait()


def emit(arrays):
    any_spec = pl.BlockSpec(memory_space=pl.ANY)
    parts = 3 * EMIT_PARTS
    return pl.pallas_call(
        emit_kernel,
        out_shape=tuple(jax.ShapeDtypeStruct(a.shape, a.dtype) for a in arrays),
        in_specs=[any_spec] * 5,
        out_specs=(any_spec,) * 5,
        scratch_shapes=[
            pltpu.VMEM((parts, EMIT_ROWS, D), BF),
            pltpu.SemaphoreType.DMA((parts,)), pltpu.SemaphoreType.DMA((2 + parts,)),
        ],
        compiler_params=pltpu.CompilerParams(vmem_limit_bytes=12 * 1024 * 1024),
        name="emit",
    )(*arrays)


def shards(activations, out_grad, gate_weight, up_weight, down_weight, step_index):
    level = step_index[0] % 4
    outs = lax.switch(
        level,
        [partial(step, i) for i in range(4)],
        activations[0], out_grad[0], gate_weight[0].T, up_weight[0].T, down_weight[0],
    )
    outs = emit(outs)
    return outs[0][None], outs[1][None], outs[2].T[None], outs[3].T[None], outs[4][None]


def solution(mesh):
    in_specs = (
        P("rep", "tp", None),
        P("rep", "tp", None),
        P("rep", None, "tp"),
        P("rep", None, "tp"),
        P("rep", "tp", None),
        P(),
    )
    out_specs = (
        P("rep", "tp", None),
        P("rep", "tp", None),
        P("rep", None, "tp"),
        P("rep", None, "tp"),
        P("rep", "tp", None),
    )
    return jax.shard_map(shards, mesh=mesh, in_specs=in_specs, out_specs=out_specs, check_vma=False)
```
